32 devices in a mesh: layer: 4 (over z), latent: 8 (over y, x, core).
Axes of the slice: x: 2, y: 2, z: 4, core: 2. Of those that a mesh axis runs over, the one named last changes fastest.
Arguments:
- harvested: bfloat16 [1024, 4, 2304], P(('layer', 'latent')), may hold values from -6 to 6
- row_order: int32 [1024], replicated, may hold values from 0 to 1023, each once
- enc_weight: bfloat16 [4, 2304, 4096], P('layer', None, 'latent'), may hold values from -0.0625 to 0.0625
- enc_bias: float32 [4096], P('latent'), may hold values from -3 to 3
- dec_weight: bfloat16 [4, 4096, 2304], P('layer', 'latent'), may hold values from -1 to 1
- dec_bias: float32 [4, 2304], P('layer'), may hold values from -3 to 3
Outputs:
- latent_codes: bfloat16 [1024, 4096], P(None, 'latent')
- loss_value: float32 [], replicated
- enc_grad: float32 [4, 2304, 4096], P('layer', None, 'latent')
- dec_grad: float32 [4, 4096, 2304], P('layer', 'latent')
The draws below stay inside these ranges and needn't reach their ends.
Inputs may be any that keep to these rules, and one draw needn't show every extreme that they name: `row_order`: each of 0 to 1023 appears exactly once.
All inputs are finite; a program needn't handle non-finite values.
Results may differ from the reference program's by a relative error of at most 0.01.
Values may be sent and summed in bfloat16 or wider, within the bound.
No kernel may reach another device: no remote copies, remote signals or barrier semaphores. Data moves between devices by JAX's collectives and lax.ppermute only.
A program may use at most 128 MiB of HBM per device.

```python
import jax
import jax.numpy as jnp
from jax import lax

D = 2304
ROWS = 1024
F = 4096
LAYERS = 4


def draw_dec_weight(key, part):
    values = jax.random.normal(jax.random.fold_in(key, 7), (LAYERS, F, D), jnp.float32)
    values = jnp.clip(values, -6.0, 6.0)
    steps = jnp.arange(LAYERS, dtype=jnp.float32) / max(LAYERS - 1, 1)
    ramp = 0.5 * 5.0 ** steps
    scaled = values * F ** (-0.5) * ramp[:, None, None]
    return jnp.clip(scaled, -1.0, 1.0).astype(jnp.bfloat16)


def levels(key, dims, shards, low, top_value):
    def one(position, parts):
        steps = jax.random.uniform(jax.random.fold_in(jax.random.fold_in(key, 6), position), (parts,), jnp.float32, low / len(shards), top_value / len(shards))
        return jnp.repeat(jnp.exp(steps), dims[position] // parts).reshape((-1,) + (1,) * (len(dims) - position - 1))

    loudness = one(*shards[0])
    for cut in shards[1:]:
        loudness = loudness * one(*cut)
    return loudness


def scatter_about(rng, dims, scale, limit, pieces=(), kind=jnp.bfloat16):
    entries = scale * jax.random.normal(rng, dims, jnp.float32)
    if pieces:
        entries = entries * levels(rng, dims, pieces, -0.22, 0.18)
    return jnp.clip(entries, -limit, limit).astype(kind)


def setup_inputs(seed: int = 0) -> dict:
    arg_keys = jax.random.split(jax.random.key(seed), 7)
    return {
        "harvested": scatter_about(arg_keys[0], (ROWS, LAYERS, D), 1.0, 6.0, ((0, 32),)),
        "row_order": jax.random.permutation(arg_keys[1], ROWS).astype(jnp.int32),
        "enc_weight": scatter_about(arg_keys[2], (LAYERS, D, F), (LAYERS * D) ** -0.5, 0.0625, ((0, 4), (2, 8))),
        "enc_bias": scatter_about(arg_keys[3], (F,), 0.5, 3.0, ((0, 8),), jnp.float32),
        "dec_weight": draw_dec_weight(jax.random.fold_in(arg_keys[6], 71), 0),
        "dec_bias": scatter_about(arg_keys[5], (LAYERS, D), 0.5, 3.0, ((0, 4),), jnp.float32),
    }


sparsity_weight = 1.0

def reference(harvested, row_order, enc_weight, enc_bias, dec_weight, dec_bias):
    inputs = harvested[row_order]
    num_rows = inputs.shape[0]
    num_layers = inputs.shape[1]
    width = inputs.shape[2]
    preact = enc_bias.astype(jnp.float32)[None, :]
    for layer_index in range(num_layers):
        preact = preact + jnp.dot(inputs[:, layer_index], enc_weight[layer_index], preferred_element_type=jnp.float32)
    latent_codes = jnp.maximum(preact, 0.0).astype(jnp.bfloat16)
    codes_wide = latent_codes.astype(jnp.float32)
    column_sums = lax.optimization_barrier(jnp.sum(codes_wide, axis=0))
    dec_wide = dec_weight.astype(jnp.float32)
    norms = jnp.sqrt(lax.optimization_barrier(jnp.sum(dec_wide * dec_wide, axis=2)) + 1e-06)
    norm_sums = lax.optimization_barrier(jnp.sum(norms, axis=0))
    squares = jnp.zeros((), jnp.float32)
    d_codes = jnp.zeros(codes_wide.shape, jnp.float32)
    dec_parts = []
    for layer_index in range(num_layers):
        rebuilt = jnp.dot(latent_codes, dec_weight[layer_index], preferred_element_type=jnp.float32)
        error_rows = rebuilt + dec_bias[layer_index][None, :] - inputs[:, layer_index].astype(jnp.float32)
        squares = squares + jnp.sum(error_rows * error_rows)
        d_recon = (2.0 / num_rows * error_rows).astype(jnp.bfloat16)
        grad_part = jnp.dot(latent_codes.T, d_recon, preferred_element_type=jnp.float32)
        grad_part = grad_part + sparsity_weight / num_rows * column_sums[:, None] * dec_wide[layer_index] / norms[layer_index][:, None]
        dec_parts.append(grad_part)
        d_codes = d_codes + jnp.dot(d_recon, dec_weight[layer_index].T, preferred_element_type=jnp.float32)
    d_codes = d_codes + sparsity_weight / num_rows * norm_sums[None, :]
    d_pre = jnp.where(latent_codes > 0, d_codes, 0.0).astype(jnp.bfloat16)
    enc_parts = []
    for layer_index in range(num_layers):
        enc_parts.append(jnp.dot(inputs[:, layer_index].T, d_pre, preferred_element_type=jnp.float32))
    loss_value = (squares + sparsity_weight * jnp.sum(codes_wide * norm_sums[None, :])) / (num_rows * num_layers * width)
    return (latent_codes, loss_value, jnp.stack(enc_parts), jnp.stack(dec_parts))
```

```python
import jax
import jax.numpy as jnp
from jax import lax
from jax.sharding import PartitionSpec as P

sparsity_weight = 1.0
chunk_count = 2


f32 = jnp.float32
bf16 = jnp.bfloat16


def log2(count):
    bits = count.bit_length() - 1
    assert 1 << bits == count
    return bits


class Hops:
    def __init__(self, layer_count, latent_count):
        self.layer_count = layer_count
        self.latent_count = latent_count
        self.layer_bits = log2(layer_count)
        self.square_bits = log2(latent_count) - 1

    def layer_mask(self, core, label):
        return label if core == 0 else reverse(label, self.layer_bits)

    def square_mask(self, core, label):
        return 2 * (label if core == 0 else reverse(label, self.square_bits))

    def layer(self, value, label):
        pairs = []
        for z in range(self.layer_count):
            for i in range(self.latent_count):
                other = z ^ self.layer_mask(i & 1, label)
                pairs.append((z * self.latent_count + i, other * self.latent_count + i))
        return lax.ppermute(value, ("layer", "latent"), pairs)

    def square(self, value, label):
        pairs = [(i, i ^ self.square_mask(i & 1, label)) for i in range(self.latent_count)]
        return lax.ppermute(value, "latent", pairs)

    def core(self, value):
        return lax.ppermute(value, "latent", [(i, i ^ 1) for i in range(self.latent_count)])


def reverse(label, bits):
    return sum(1 << (bits - 1 - t) for t in range(bits) if label >> t & 1)


def gather(exchange, bits, block, total=None):
    blocks = block[None]
    for t in range(bits):
        if total is not None:
            blocks, total = lax.optimization_barrier((blocks, total))
            total = total + exchange(total, 1 << t)
        blocks = jnp.concatenate([blocks, exchange(blocks, 1 << t)], axis=0)
    return blocks if total is None else (blocks, total)


def after(value, gate):
    return lax.optimization_barrier((value, gate))[0]


def scatter(exchange, bits, blocks):
    blocks = list(blocks)
    for t in reversed(range(bits)):
        keep = 1 << t
        other = exchange(jnp.stack(blocks[keep:]), keep)
        kind = blocks[0].dtype
        total = [blocks[n].astype(f32) + other[n].astype(f32) for n in range(keep)]
        blocks = [b.astype(kind) for b in total]
    return total[0]


def on_device(harvested, row_order, enc_weight, enc_bias, dec_weight, dec_bias):
    layer_count = lax.axis_size("layer")
    latent_count = lax.axis_size("latent")
    hops = Hops(layer_count, latent_count)
    layer_index = lax.axis_index("layer")
    latent_index = lax.axis_index("latent")
    core = latent_index & 1
    owner_rows, _, width = harvested.shape
    latents = enc_weight.shape[2]
    num_rows = row_order.shape[0]
    half_latent = latent_count // 2
    rows = owner_rows // chunk_count
    enc = enc_weight[0]
    dec = dec_weight[0]
    swap = [reverse(j, hops.layer_bits) for j in range(layer_count)]

    slabs = []
    for label in range(layer_count):
        mask = jnp.where(core == 0, hops.layer_mask(0, label), hops.layer_mask(1, label))
        slab = lax.dynamic_slice_in_dim(harvested, layer_index ^ mask, 1, 1)
        slabs.append(slab.reshape(owner_rows, width))

    dec_wide = dec.astype(f32)
    norms = jnp.sqrt(jnp.sum(dec_wide * dec_wide, axis=1) + 1e-06)

    flat = half_latent * layer_count * rows
    contract_rows = (((0,), (0,)), ((), ()))
    contract_width = (((1,), (1,)), ((), ()))

    def by_label(own, other):
        own = own.reshape(half_latent, layer_count, rows, latents)
        other = other.reshape(half_latent, layer_count, rows, latents)
        return [jnp.stack([own[:, j], other[:, swap[j]]]) for j in range(layer_count)]

    def in_order(blocks):
        own = jnp.moveaxis(blocks[:, 0], 0, 1).reshape(flat, latents)
        other = jnp.stack([blocks[swap[j], 1] for j in range(layer_count)], axis=1)
        return own, other.reshape(flat, latents)

    x_parts, code_parts, recon_parts, pre_parts = [], [], [], []
    square_part = jnp.zeros((), f32)
    for chunk in range(chunk_count):
        here = [s[chunk * rows : (chunk + 1) * rows] for s in slabs]
        here = here[:1] + [hops.layer(s, j) for j, s in enumerate(here) if j]
        piece = jnp.stack(here)
        x_own = gather(hops.square, hops.square_bits, piece).reshape(flat, width)
        x_other = hops.core(x_own)
        partial = [jnp.dot(x, enc, preferred_element_type=f32) for x in (x_own, x_other)]
        if chunk:
            partial = after(partial, own_codes)
        pre = scatter(hops.layer, hops.layer_bits, by_label(*partial))
        own_codes = jnp.maximum(pre + enc_bias, 0.0).astype(bf16)
        if chunk == 0:
            codes, norm_sums = gather(hops.layer, hops.layer_bits, own_codes, norms)
        else:
            codes = gather(hops.layer, hops.layer_bits, own_codes)
        codes = in_order(codes)
        code_parts += codes
        sent = jnp.dot(codes[1], dec, preferred_element_type=f32).astype(bf16)
        came = hops.core(sent)
        sums = jnp.dot(codes[0], dec, preferred_element_type=f32) + came.astype(f32)
        sums = sums.astype(bf16).reshape(half_latent, layer_count, rows, width)
        rebuilt = scatter(hops.square, hops.square_bits, sums)
        error = rebuilt + dec_bias[0] - piece.astype(f32)
        square_part = square_part + jnp.sum(error * error)
        d_block = (2.0 / num_rows * error).astype(bf16)
        if chunk < chunk_count - 1:
            d_own = gather(hops.square, hops.square_bits, d_block)
        else:
            codes_all = jnp.concatenate(code_parts, axis=0)
            column_sums = jnp.sum(codes_all.astype(f32), axis=0)
            sparse_part = jnp.where(
                layer_index == 0, sparsity_weight * jnp.sum(column_sums * norm_sums), 0.0
            )
            loss_total = (square_part + sparse_part)[None]
            d_own, loss_total = gather(hops.square, hops.square_bits, d_block, loss_total)
            d_own, loss_total = lax.optimization_barrier((d_own, loss_total))
            loss_total = loss_total + hops.core(loss_total)
        d_own = d_own.reshape(flat, width)
        d_other = hops.core(d_own)
        partial = [
            lax.dot_general(d, dec, contract_width, preferred_element_type=f32).astype(bf16)
            for d in (d_own, d_other)
        ]
        d_codes = scatter(hops.layer, hops.layer_bits, by_label(*partial))
        d_codes = d_codes + sparsity_weight / num_rows * norm_sums
        own_pre = jnp.where(own_codes > 0, d_codes, 0.0).astype(bf16)
        if chunk < chunk_count - 1:
            d_pre = gather(hops.layer, hops.layer_bits, own_pre)
        else:
            d_pre, loss_total = gather(hops.layer, hops.layer_bits, own_pre, loss_total)
        d_pre = in_order(d_pre)
        x_parts += [x_own, x_other]
        recon_parts += [d_own, d_other]
        pre_parts += d_pre

    dec_grad = lax.dot_general(
        codes_all,
        jnp.concatenate(recon_parts, axis=0),
        contract_rows,
        preferred_element_type=f32,
    )
    dec_grad = dec_grad + (sparsity_weight / num_rows * column_sums / norms)[:, None] * dec_wide
    enc_grad = lax.dot_general(
        jnp.concatenate(x_parts, axis=0),
        jnp.concatenate(pre_parts, axis=0),
        contract_rows,
        preferred_element_type=f32,
    )

    owner = row_order // owner_rows
    within = row_order % owner_rows
    apart_latent = (owner % latent_count) ^ latent_index
    apart_layer = (owner // latent_count) ^ layer_index
    other_core = apart_latent & 1
    turned = (core ^ other_core) == 1
    place = (within // rows) * 2 + other_core
    for apart, bits in ((apart_latent >> 1, hops.square_bits), (apart_layer, hops.layer_bits)):
        label = jnp.zeros_like(apart)
        for t in range(bits):
            source = jnp.where(turned, bits - 1 - t, t)
            label = label + (((apart >> source) & 1) << t)
        place = place * (1 << bits) + label
    place = place * rows + within % rows
    choose = (place[:, None] == jnp.arange(num_rows, dtype=jnp.int32)[None, :]).astype(bf16)
    latent_codes = jnp.dot(choose, codes_all, preferred_element_type=f32).astype(bf16)

    loss_value = loss_total[0] / (num_rows * layer_count * width)
    return (latent_codes, loss_value, enc_grad[None], dec_grad[None])


def solution(mesh):
    in_specs = (
        P(("layer", "latent"), None, None),
        P(),
        P("layer", None, "latent"),
        P("latent"),
        P("layer", "latent", None),
        P("layer", None),
    )
    out_specs = (P(None, "latent"), P(), P("layer", None, "latent"), P("layer", "latent", None))
    return jax.shard_map(
        on_device, mesh=mesh, in_specs=in_specs, out_specs=out_specs, check_vma=False
    )
```
